32 devices in a mesh: grp: 2 (over x), gx: 16 (over z, y, core).
Axes of the slice: x: 2, y: 2, z: 4, core: 2. Of those that a mesh axis runs over, the one named last changes fastest.
Arguments:
- voltages: bfloat16 [1024, 143360], P(('grp', 'gx')), parts along dimension 0, may hold values from -6 to 6
- taps: float32 [4, 4096], replicated, may hold values from -3 to 3
- weights: bfloat16 [2, 64, 256, 128], P(None, 'gx'), may hold values from -0.25 to 0.25
- antenna_weight_index: int32 [1024], P(('grp', 'gx')), parts along dimension 0, may hold values from 0 to 255
- flagged: int32 [1024], P(('grp', 'gx')), parts along dimension 0, may hold values 0 or 1
- trials: int32 [256], P(('grp', 'gx')), parts along dimension 0, may hold values from 0 to 63
Outputs:
- dedispersed: float32 [2, 32, 256, 64], P(None, None, ('grp', 'gx')), parts along dimension 2
The draws below stay inside these ranges and needn't reach their ends.
There are 2 independent parts, one for each index of `grp`. The reference program is written for one: setup_inputs(seed, part) draws one part's arguments, and reference() takes and returns one part's arrays. A program takes and returns all parts, laid end to end along the dimension named above; an argument that names none is the same for every part. Nothing has to cross between parts.
All inputs are finite; a program needn't handle non-finite values. No bound on the sum of `flagged` on one device may be relied on, other than what follows from the above.
Results may differ from the reference program's by a relative error of at most 0.009.
Values may be sent and summed in bfloat16 or wider, within the bound.
A program may use at most 64 MiB of HBM per device.

```python
import math
import jax
import jax.numpy as jnp
from jax import lax

FRAME_COUNT = 32
FORWARD_LENGTH = 4096
TAP_COUNT = 4
CH_LO = 1024
WEIGHT_ROWS = 256
ANTENNA_COUNT = 512
CHANNEL_COUNT = 64
BEAM_COUNT = 128
SAMPLE_COUNT = 143360


def place_ends(drawn, key, least, high):
    spot = [jax.random.randint(jax.random.fold_in(key, axis), (), 0, length) for axis, length in enumerate(drawn.shape)]
    widest = drawn.shape.index(max(drawn.shape))
    next_to = spot[:widest] + [(spot[widest] + 1) % drawn.shape[widest]] + spot[widest + 1:]
    return drawn.at[tuple(spot)].set(least).at[tuple(next_to)].set(high)


def steps_of(stream_key, extent, split, least, high):
    loudness, own = 1.0, jax.random.fold_in(stream_key, 6)
    for axis_at, shards_of in split:
        draws = jnp.exp(jax.random.uniform(jax.random.fold_in(own, axis_at), (shards_of,), jnp.float32, least / len(split), high / len(split)))
        loudness = loudness * jnp.repeat(draws, extent[axis_at] // shards_of).reshape([-1 if axis == axis_at else 1 for axis in range(len(extent))])
    return loudness


def gaussian(stream_key, dims, width, most, pieces=(), kind=jnp.bfloat16):
    array = width * jax.random.normal(stream_key, dims, jnp.float32)
    if pieces:
        array = array * steps_of(stream_key, dims, pieces, -0.22, 0.18)
    return jnp.clip(array, -most, most).astype(kind)


def setup_inputs(seed: int = 0, part: int = 0) -> dict:
    key_of = jax.random.split(jax.random.key(seed), 7)
    part_keys = jax.random.split(jax.random.fold_in(key_of[6], part), 7)
    voltages = gaussian(part_keys[0], (ANTENNA_COUNT, SAMPLE_COUNT), 1.0, 6.0, ((0, 16),))
    taps = gaussian(key_of[1], (TAP_COUNT, FORWARD_LENGTH), 0.5, 3.0, (), jnp.float32)
    weights = gaussian(key_of[2], (2, CHANNEL_COUNT, WEIGHT_ROWS, BEAM_COUNT), ANTENNA_COUNT ** -0.5, 0.25, ((1, 16),))
    antenna_weight_index = place_ends(jax.random.randint(part_keys[3], (ANTENNA_COUNT,), 0, WEIGHT_ROWS), jax.random.fold_in(part_keys[3], 1), 0, WEIGHT_ROWS - 1).astype(jnp.int32)
    flagged = place_ends((jax.random.randint(part_keys[4], (ANTENNA_COUNT,), 0, 8) < 1).astype(jnp.int32), jax.random.fold_in(part_keys[4], 1), 0, 1)
    trials = place_ends(jax.random.randint(part_keys[5], (BEAM_COUNT,), 0, 64), jax.random.fold_in(part_keys[5], 1), 0, 63).astype(jnp.int32)
    return dict(voltages=voltages, taps=taps, weights=weights, antenna_weight_index=antenna_weight_index, flagged=flagged, trials=trials)


dm_unit = 0.173


def forward_table(nfft_len, first_bin, kept):
    bins = first_bin + jnp.arange(kept, dtype=jnp.int32)
    samples = jnp.arange(nfft_len, dtype=jnp.int32)
    modulo = (bins[:, None] * samples[None, :]) % nfft_len
    angles = modulo.astype(jnp.float32) * (2.0 * math.pi / nfft_len)
    return jnp.concatenate([jnp.cos(angles), -jnp.sin(angles)], 0).astype(jnp.bfloat16)


def inverse_table(length):
    chans = jnp.arange(length, dtype=jnp.int32)
    modulo = (chans[:, None] * chans[None, :]) % length
    angles = modulo.astype(jnp.float32) * (2.0 * math.pi / length)
    cosine = jnp.cos(angles)
    sine = jnp.sin(angles)
    return jnp.stack([jnp.stack([cosine, sine], 1), jnp.stack([-sine, cosine], 1)], 0).astype(jnp.bfloat16)


def filter_frames(frame_samples, taps):
    frames = frame_samples.shape[1] - taps.shape[0] + 1
    running_sum = jnp.zeros((frame_samples.shape[0], frames, frame_samples.shape[2]), jnp.float32)
    for tap_index in range(taps.shape[0]):
        running_sum = running_sum + taps[tap_index].astype(jnp.float32)[None, None, :] * frame_samples[:, tap_index:tap_index + frames].astype(jnp.float32)
    return running_sum.astype(jnp.bfloat16)


def chirp_apply(beams, trial_ids, chan_start, channel_total):
    chans = (chan_start + jnp.arange(beams.shape[3], dtype=jnp.int32)).astype(jnp.float32) / channel_total
    phase = (-2.0 * math.pi * dm_unit) * (trial_ids.astype(jnp.float32) + 1.0)[:, None] * (chans * chans)[None, :]
    cosine = jnp.cos(phase)[None]
    sine = jnp.sin(phase)[None]
    real_part = beams[0].astype(jnp.float32)
    imag_part = beams[1].astype(jnp.float32)
    return jnp.stack([real_part * cosine - imag_part * sine, real_part * sine + imag_part * cosine]).astype(jnp.bfloat16)


def reference(voltages, taps, weights, antenna_weight_index, flagged, trials):
    highest = lax.Precision.HIGHEST
    fwd = forward_table(FORWARD_LENGTH, CH_LO, CHANNEL_COUNT).astype(jnp.float32)
    channel_keep_mask = (1 - flagged).astype(jnp.float32)
    antenna_group = math.gcd(ANTENNA_COUNT, 64)
    frame_samples = voltages.reshape(ANTENNA_COUNT // antenna_group, antenna_group, FRAME_COUNT + TAP_COUNT - 1, FORWARD_LENGTH)
    kept_channels = channel_keep_mask.reshape(ANTENNA_COUNT // antenna_group, antenna_group)

    def spectrum(item):
        volts, kept = item
        filtered = filter_frames(volts, taps)
        result = jnp.einsum("afn,kn->kfa", filtered.astype(jnp.float32), fwd, precision=highest)
        return (result * (FORWARD_LENGTH ** -0.5) * kept[None, None, :]).astype(jnp.bfloat16)

    partial_outputs = lax.map(spectrum, (frame_samples, kept_channels))
    frame_spectra = jnp.transpose(partial_outputs, (1, 2, 0, 3)).reshape(2, CHANNEL_COUNT, FRAME_COUNT, ANTENNA_COUNT)
    onehot = (antenna_weight_index[:, None] == jnp.arange(WEIGHT_ROWS, dtype=jnp.int32)[None, :]).astype(jnp.float32)
    sums = jnp.einsum("rcfa,at->rcft", frame_spectra.astype(jnp.float32), onehot, precision=highest)
    wfloat = weights.astype(jnp.float32)

    def product(left, right):
        return jnp.einsum("cft,ctb->fbc", left, right, precision=highest)

    real_part = product(sums[0], wfloat[0]) - product(sums[1], wfloat[1])
    imag_part = product(sums[0], wfloat[1]) + product(sums[1], wfloat[0])
    beams = jnp.stack([real_part, imag_part]).astype(jnp.bfloat16)
    chirped = chirp_apply(beams, trials, 0, CHANNEL_COUNT)
    inv = inverse_table(CHANNEL_COUNT).astype(jnp.float32)
    result = jnp.einsum("rfbc,rcsd->sfbd", chirped.astype(jnp.float32), inv, precision=highest)
    return result * (CHANNEL_COUNT ** -0.5)
```

```python
import functools
import math

import jax
import jax.numpy as jnp
import numpy as np
from jax import lax
from jax.experimental import pallas as pl
from jax.experimental.pallas import tpu as pltpu
from jax.sharding import PartitionSpec as P

FRAME_COUNT = 32
FORWARD_LENGTH = 4096
TAP_COUNT = 4
CH_LO = 1024
WEIGHT_ROWS = 256
LANES = 128
SUBLANES = 16
DM_UNIT = 0.173
MESH = pl.DeviceIdType.MESH
VMEM_BYTES = 67108864
GROUPS = (8, 8, 8, 8)
K_TILE = 256


def forward_columns(channels, owners):
    local = channels // owners
    kept = np.arange(channels).reshape(owners, 1, local)
    bins = np.broadcast_to(CH_LO + kept, (owners, 2, local)).reshape(-1)
    part = np.broadcast_to(np.arange(2).reshape(1, 2, 1), (owners, 2, local)).reshape(-1)
    angle = (np.arange(FORWARD_LENGTH)[:, None] * bins[None] % FORWARD_LENGTH) * (2.0 * math.pi / FORWARD_LENGTH)
    return np.where(part[None] == 0, np.cos(angle), -np.sin(angle)).astype(jnp.bfloat16)


def inverse_rows(channels, owners):
    local = channels // owners
    chan = (np.arange(owners)[None, :] * local + np.arange(local)[:, None]).reshape(1, -1, 1)
    angle = (chan * np.arange(channels) % channels) * (2.0 * math.pi / channels)
    cosine, sine = np.cos(angle), np.sin(angle)
    real = np.concatenate([cosine, -sine], 0)
    imag = np.concatenate([sine, cosine], 0)
    return np.stack([real, imag]).reshape(2, 2 * channels, channels).astype(jnp.bfloat16)


def kernel(
    n, index_hbm, flagged_hbm, trials_hbm, volts_hbm, taps_hbm, table_hbm, weights_hbm, inverse_hbm, out,
    index, flagged, trials, volts, taps, table, weights, inverse,
    wide_taps, keep, chirp, index_rows, spec,
    got_index, got_spec, gathered, lined, sending, got_beams, turned, stacked,
    load_sems, remote_sems,
):
    me = lax.axis_index("gx")
    antennas = volts.shape[0]
    locals_ = weights.shape[1]
    beam_total = weights.shape[3]
    channels = n * locals_
    rows = 2 * channels
    frames = FRAME_COUNT
    quad = LANES // antennas
    parts = 2 * locals_
    half = LANES // parts
    halves = frames // half
    beams = beam_total // n
    steps = len(GROUPS)

    barrier = pltpu.get_barrier_semaphore()
    for d in range(1, n):
        pl.semaphore_signal(barrier, inc=1, device_id={"gx": lax.rem(me + d, n)}, device_id_type=MESH)

    def load(source, target, at):
        return pltpu.make_async_copy(source, target, load_sems.at[at])

    streams = []
    for at in range(steps):
        begin = sum(GROUPS[:at]) + (TAP_COUNT - 1 if at else 0)
        end = sum(GROUPS[: at + 1]) + TAP_COUNT - 1
        span = pl.ds(begin * FORWARD_LENGTH, (end - begin) * FORWARD_LENGTH)
        streams.append(load(volts_hbm.at[:, span], volts.at[:, span], at))
    load_taps = load(taps_hbm, taps, steps)
    load_table = load(table_hbm, table, steps + 1)
    load_weights = load(weights_hbm, weights, steps + 2)
    load_inverse = load(inverse_hbm, inverse, steps + 3)
    load_index = load(index_hbm, index, steps + 4)
    load_flagged = load(flagged_hbm, flagged, steps + 5)
    load_trials = load(trials_hbm, trials, steps + 6)
    for one in (load_taps, load_table, streams[0], load_index, load_flagged, load_trials):
        one.start()
    streams[1].start()

    def copies(source, target, send, recv):
        for d in range(1, n):
            peer = lax.rem(me + d, n)
            pltpu.make_async_remote_copy(
                src_ref=source(peer),
                dst_ref=target(me),
                send_sem=send,
                recv_sem=recv,
                device_id={"gx": peer},
                device_id_type=MESH,
            ).start()

    def whole(source, target, send, recv):
        others = pl.ds(0, n - 1)
        return pltpu.make_async_remote_copy(
            src_ref=source(others),
            dst_ref=target(others),
            send_sem=send,
            recv_sem=recv,
            device_id={"gx": lax.rem(me + 1, n)},
            device_id_type=MESH,
        )

    index_args = (lambda p: index_rows.at[p], lambda p: got_index.at[p], remote_sems.at[0], remote_sems.at[1])

    def spans(at):
        return sum(GROUPS[:at]) // quad, sum(GROUPS[: at + 1]) // quad

    def piece_args(at):
        first, last = spans(at)
        span = pl.ds(first * LANES, (last - first) * LANES)
        return (
            lambda p: spec.at[p, :, span], lambda p: got_spec.at[p, :, span],
            remote_sems.at[2 + 2 * at], remote_sems.at[3 + 2 * at],
        )

    def beam_args(h):
        return (
            lambda p: sending.at[h, p], lambda p: got_beams.at[h, p],
            remote_sems.at[2 + 2 * (steps + h)], remote_sems.at[3 + 2 * (steps + h)],
        )

    load_taps.wait()
    for tap in range(TAP_COUNT):
        wide_taps[tap] = jnp.broadcast_to(taps[tap : tap + 1, :], (SUBLANES, FORWARD_LENGTH)).astype(jnp.bfloat16)

    def filtered(at, k):
        span = slice(k * K_TILE, (k + 1) * K_TILE)
        tap = [wide_taps[j, :, span] for j in range(TAP_COUNT)]
        first = sum(GROUPS[:at])
        pieces = []
        for block in range(antennas // SUBLANES):
            x = [
                volts[
                    block * SUBLANES : (block + 1) * SUBLANES,
                    f * FORWARD_LENGTH + k * K_TILE : f * FORWARD_LENGTH + (k + 1) * K_TILE,
                ]
                for f in range(first, first + GROUPS[at] + TAP_COUNT - 1)
            ]
            pieces.append(
                [
                    (x[f] * tap[0] + x[f + 1] * tap[1]) + (x[f + 2] * tap[2] + x[f + 3] * tap[3])
                    for f in range(GROUPS[at])
                ]
            )
        return jnp.concatenate([piece[f] for f in range(GROUPS[at]) for piece in pieces], 0)

    def emit(at, total):
        first, last = spans(at)
        eights = LANES // parts
        for tile in range(first, last):
            block = total[(tile - first) * LANES : (tile - first + 1) * LANES]
            for part in range(rows // LANES):
                across = (block[:, part * LANES : (part + 1) * LANES] * keep[...]).T
                spec[part * eights : (part + 1) * eights, :, tile * LANES : (tile + 1) * LANES] = across.reshape(
                    eights, parts, LANES
                ).astype(jnp.bfloat16)

    def small():
        load_index.wait()
        load_flagged.wait()
        lane_one = lax.broadcasted_iota(jnp.int32, (1, LANES), 1) % antennas
        row = jnp.zeros((1, LANES), jnp.int32)
        for a in range(antennas):
            row = jnp.where(lane_one == a, index[a], row)
        index_rows[...] = jnp.broadcast_to(row[None], index_rows.shape)
        antenna = lax.broadcasted_iota(jnp.int32, (antennas, LANES), 0)
        off = jnp.zeros((antennas, LANES), jnp.int32)
        for a in range(antennas):
            off = jnp.where(antenna == a, flagged[a], off)
        kept = (1 - off).astype(jnp.float32) * FORWARD_LENGTH ** (-0.5)
        for q in range(quad):
            keep[q * antennas : (q + 1) * antennas, :] = kept

    def turn():
        load_trials.wait()
        beam = lax.broadcasted_iota(jnp.int32, (beams, LANES), 0)
        trial = jnp.zeros((beams, LANES), jnp.int32)
        for b in range(beams):
            trial = jnp.where(beam == b, trials[b], trial)
        scaled = (-2.0 * math.pi * DM_UNIT) * (trial.astype(jnp.float32) + 1.0)
        lane = lax.broadcasted_iota(jnp.int32, (n, beams, LANES), 2)
        owner = lax.broadcasted_iota(jnp.int32, (n, beams, LANES), 0)
        chan = (owner * locals_ + lane // half % locals_).astype(jnp.float32) / channels
        phase = scaled[None] * (chan * chan)
        chirp[0] = jnp.cos(phase)
        chirp[1] = jnp.where(lane < LANES // 2, -1.0, 1.0) * jnp.sin(phase)

    def gather_weights():
        whole(*index_args).wait_recv()
        load_weights.wait()
        lane = lax.broadcasted_iota(jnp.int32, (LANES, LANES), 1)
        lane_quad = lax.broadcasted_iota(jnp.int32, (1, LANES), 1) // antennas
        blocks = []
        for ag in range(n // quad):
            row = got_index[ag * quad]
            for q in range(1, quad):
                row = jnp.where(lane_quad == q, got_index[ag * quad + q], row)
            column = jnp.broadcast_to(row.astype(jnp.float32), (LANES, LANES)).T.astype(jnp.int32)
            blocks.append(
                jnp.concatenate(
                    [
                        jnp.where(column == lane + t * LANES, 1.0, 0.0).astype(jnp.bfloat16)
                        for t in range(WEIGHT_ROWS // LANES)
                    ],
                    1,
                )
            )
        onehot = jnp.concatenate(blocks, 0)
        for c in range(locals_):
            both = jnp.concatenate([weights[0, c], weights[1, c]], 1)
            gathered[c] = jnp.dot(onehot, both, preferred_element_type=jnp.float32).astype(jnp.bfloat16)

    load_table.wait()
    for at in range(steps):
        streams[at].wait()
        if at + 2 < steps:
            streams[at + 2].start()
        elif at + 2 == steps:
            load_weights.start()
            load_inverse.start()
        if at == 0:
            small()
        total = None
        for k in range(FORWARD_LENGTH // K_TILE):
            part = jnp.dot(
                filtered(at, k), table[k * K_TILE : (k + 1) * K_TILE, :], preferred_element_type=jnp.float32
            )
            total = part if total is None else total + part
        emit(at, total)
        if at == 0:
            pl.semaphore_wait(barrier, n - 1)
            copies(*index_args)
            got_index[me] = index_rows[0]
        copies(*piece_args(at))
    turn()
    got_spec[me] = spec[me]
    gather_weights()

    lane_part = lax.broadcasted_iota(jnp.int32, (parts, LANES), 1) // antennas

    def line(at):
        whole(*piece_args(at)).wait_recv()
        for sg in range(n // quad):
            for ft in range(*spans(at)):
                pieces = [
                    got_spec[sg * quad + s, :, ft * LANES : (ft + 1) * LANES].astype(jnp.float32)
                    for s in range(quad)
                ]
                for f in range(quad):
                    made = None
                    for s in range(quad):
                        piece = pieces[s]
                        if s != f:
                            piece = pltpu.roll(piece, ((s - f) * antennas) % LANES, 1)
                        made = piece if made is None else jnp.where(lane_part == s, piece, made)
                    to = (ft * quad + f) * parts
                    lined[sg, to : to + parts, :] = made

    def product(h):
        real, imag = [], []
        for c in range(locals_):
            left = jnp.concatenate(
                [
                    jnp.concatenate(
                        [
                            lined[sg, pl.ds(h * half * parts + r * locals_ + c, half, stride=parts), :]
                            for sg in range(n // quad)
                        ],
                        1,
                    )
                    for r in range(2)
                ],
                0,
            ).astype(jnp.bfloat16)
            both = jnp.dot(left, gathered[c], preferred_element_type=jnp.float32)
            real.append(both[:half, :beam_total] - both[half:, beam_total:])
            imag.append(both[:half, beam_total:] + both[half:, :beam_total])
        stack = jnp.concatenate(real + imag, 0)
        owners = LANES // beams
        for bt in range(beam_total // LANES):
            across = stack[:, bt * LANES : (bt + 1) * LANES].T
            sending[h, bt * owners : (bt + 1) * owners] = across.reshape(owners, beams, LANES).astype(jnp.bfloat16)

    def finish(h):
        whole(*beam_args(h)).wait_recv()
        for s in range(n):
            block = got_beams[h, s].astype(jnp.float32)
            swapped = pltpu.roll(block, LANES // 2, 1)
            turned[pl.ds(s, beams, stride=n), :] = block * chirp[0, s] + swapped * chirp[1, s]
        each = LANES // n
        deep = parts // each
        place = lax.broadcasted_iota(jnp.int32, (half, LANES), 1) // n
        for g in range(beams // each):
            across = turned[g * LANES : (g + 1) * LANES, :].T
            for b in range(each):
                for k in range(deep):
                    made = None
                    for slot in range(each):
                        piece = across[(k * each + slot) * half : (k * each + slot + 1) * half]
                        if b != slot:
                            piece = pltpu.roll(piece, ((slot - b) * n) % LANES, 1)
                        made = piece if made is None else jnp.where(place == slot, piece, made)
                    stacked[k, pl.ds(g * each + b, half, stride=beams), :] = made
        left = jnp.concatenate([stacked[k] for k in range(deep)], 1).astype(jnp.bfloat16)
        for s in range(2):
            total = jnp.dot(left, inverse[s], preferred_element_type=jnp.float32) * channels ** (-0.5)
            out[s, h * half : (h + 1) * half] = total.reshape(half, beams, channels)

    done = 0
    for h in range(halves):
        while done < steps and sum(GROUPS[:done]) < (h + 1) * half:
            line(done)
            done += 1
        product(h)
        copies(*beam_args(h))
        got_beams[h, me] = sending[h, me]
    load_inverse.wait()
    whole(*index_args).wait_send()
    for at in range(steps):
        whole(*piece_args(at)).wait_send()
    for h in range(halves):
        finish(h)
        whole(*beam_args(h)).wait_send()


def per_device(voltages, taps, weights, antenna_weight_index, flagged, trials):
    n = lax.axis_size("gx")
    locals_ = weights.shape[1]
    beam_total = weights.shape[3]
    channels = locals_ * n
    antennas = voltages.shape[0]
    beams = trials.shape[0]
    parts = 2 * locals_
    rows = 2 * channels
    half = LANES // parts
    halves = FRAME_COUNT // half
    steps = len(GROUPS)
    table = forward_columns(channels, n)
    inverse = inverse_rows(channels, n)
    room = 2 * FRAME_COUNT * beams * max(channels, LANES) * 4 + (1 << 17)
    hbm = pl.BlockSpec(memory_space=pltpu.HBM)
    return pl.pallas_call(
        functools.partial(kernel, n),
        out_shape=pltpu.VMEM((2, FRAME_COUNT, beams, channels), jnp.float32),
        in_specs=[hbm] * 8,
        out_specs=pl.BlockSpec(memory_space=pltpu.VMEM),
        scratch_shapes=[
            pltpu.SMEM(antenna_weight_index.shape, jnp.int32),
            pltpu.SMEM(flagged.shape, jnp.int32),
            pltpu.SMEM(trials.shape, jnp.int32),
            pltpu.VMEM(voltages.shape, jnp.bfloat16),
            pltpu.VMEM(taps.shape, jnp.float32),
            pltpu.VMEM(table.shape, jnp.bfloat16),
            pltpu.VMEM(weights.shape, jnp.bfloat16),
            pltpu.VMEM(inverse.shape, jnp.bfloat16),
            pltpu.VMEM((TAP_COUNT, SUBLANES, FORWARD_LENGTH), jnp.bfloat16),
            pltpu.VMEM((LANES, LANES), jnp.float32),
            pltpu.VMEM((2, n, beams, LANES), jnp.float32),
            pltpu.VMEM((n, 1, LANES), jnp.int32),
            pltpu.VMEM((n, parts, FRAME_COUNT * antennas), jnp.bfloat16),
            pltpu.VMEM((n, 1, LANES), jnp.int32),
            pltpu.VMEM((n, parts, FRAME_COUNT * antennas), jnp.bfloat16),
            pltpu.VMEM((locals_, n * antennas, 2 * beam_total), jnp.bfloat16),
            pltpu.VMEM((n * antennas // LANES, FRAME_COUNT * parts, LANES), jnp.float32),
            pltpu.VMEM((halves, n, beams, LANES), jnp.bfloat16),
            pltpu.VMEM((halves, n, beams, LANES), jnp.bfloat16),
            pltpu.VMEM((beams * n, LANES), jnp.float32),
            pltpu.VMEM((rows // LANES, half * beams, LANES), jnp.float32),
            pltpu.SemaphoreType.DMA((steps + 7,)),
            pltpu.SemaphoreType.DMA((2 * (1 + steps + halves),)),
        ],
        compiler_params=pltpu.CompilerParams(
            collective_id=0, has_side_effects=True, vmem_limit_bytes=VMEM_BYTES - room
        ),
        name="beamformer",
    )(
        antenna_weight_index, flagged, trials, voltages, taps,
        jnp.asarray(table), weights, jnp.asarray(inverse),
    )


def solution(mesh):
    return jax.shard_map(
        per_device,
        mesh=mesh,
        in_specs=(
            P(("grp", "gx"), None),
            P(),
            P(None, "gx", None, None),
            P(("grp", "gx")),
            P(("grp", "gx")),
            P(("grp", "gx")),
        ),
        out_specs=P(None, None, ("grp", "gx"), None),
        check_vma=False,
    )
```

```python
import functools
import math

import jax
import jax.numpy as jnp
import numpy as np
from jax import lax
from jax.experimental import pallas as pl
from jax.experimental.pallas import tpu as pltpu
from jax.sharding import PartitionSpec as P

FRAME_COUNT = 32
FORWARD_LENGTH = 4096
TAP_COUNT = 4
CH_LO = 1024
WEIGHT_ROWS = 256
LANES = 128
SUBLANES = 16
DM_UNIT = 0.173
MESH = pl.DeviceIdType.MESH
NT = (((1,), (1,)), ((), ()))
VMEM_BYTES = 67108864
GROUPS = (8, 8, 8, 8)
K_TILE = 256


def forward_rows(channels, owners):
    local = channels // owners
    kept = np.arange(channels).reshape(owners, 1, local)
    bins = np.broadcast_to(CH_LO + kept, (owners, 2, local)).reshape(-1)
    part = np.broadcast_to(np.arange(2).reshape(1, 2, 1), (owners, 2, local)).reshape(-1)
    angle = (bins[:, None] * np.arange(FORWARD_LENGTH)[None] % FORWARD_LENGTH) * (2.0 * math.pi / FORWARD_LENGTH)
    return np.where(part[:, None] == 0, np.cos(angle), -np.sin(angle)).astype(jnp.bfloat16)


def inverse_rows(channels, owners):
    local = channels // owners
    chan = (np.arange(owners)[None, :] * local + np.arange(local)[:, None]).reshape(1, -1, 1)
    angle = (chan * np.arange(channels) % channels) * (2.0 * math.pi / channels)
    cosine, sine = np.cos(angle), np.sin(angle)
    real = np.concatenate([cosine, -sine], 0)
    imag = np.concatenate([sine, cosine], 0)
    return np.stack([real, imag]).reshape(2, 2 * channels, channels).astype(jnp.bfloat16)


def kernel(
    n, index_hbm, flagged_hbm, trials_hbm, volts_hbm, taps_hbm, table_hbm, weights_hbm, inverse_hbm, out,
    index, flagged, trials, volts, taps, table, weights, inverse,
    wide_taps, keep, chirp, index_rows, spec,
    got_index, got_spec, gathered, partial, lined, sending, got_beams, turned,
    load_sems, remote_sems, spec_sems,
):
    me = lax.axis_index("gx")
    mine = me // (n // 2)
    yours = 1 - mine
    antennas = volts.shape[0]
    locals_ = weights.shape[1]
    beam_total = weights.shape[3]
    channels = n * locals_
    rows = 2 * channels
    frames = FRAME_COUNT
    quad = LANES // antennas
    parts = 2 * locals_
    half = LANES // parts
    halves = frames // half
    beams = beam_total // n
    steps = len(GROUPS)

    barrier = pltpu.get_barrier_semaphore()
    for d in range(1, n):
        pl.semaphore_signal(barrier, inc=1, device_id={"gx": lax.rem(me + d, n)}, device_id_type=MESH)

    def load(source, target, at):
        return pltpu.make_async_copy(source, target, load_sems.at[at])

    streams = []
    for at in range(steps):
        begin = sum(GROUPS[:at]) + (TAP_COUNT - 1 if at else 0)
        end = sum(GROUPS[: at + 1]) + TAP_COUNT - 1
        span = pl.ds(begin * FORWARD_LENGTH, (end - begin) * FORWARD_LENGTH)
        streams.append(load(volts_hbm.at[:, span], volts.at[:, span], at))
    load_taps = load(taps_hbm, taps, steps)
    load_table = load(table_hbm, table, steps + 1)
    load_weights = load(weights_hbm, weights, steps + 2)
    load_inverse = load(inverse_hbm, inverse, steps + 3)
    load_index = load(index_hbm, index, steps + 4)
    load_flagged = load(flagged_hbm, flagged, steps + 5)
    load_trials = load(trials_hbm, trials, steps + 6)
    for one in (load_taps, load_table, streams[0], load_index, load_flagged, load_trials):
        one.start()
    for one in streams[1:] + [load_weights, load_inverse]:
        one.start()
    peers = [lax.rem(me + d, n) for d in range(n)]

    def copies(source, target, send, recv):
        for peer in peers[1:]:
            pltpu.make_async_remote_copy(
                src_ref=source(peer),
                dst_ref=target(me),
                send_sem=send,
                recv_sem=recv,
                device_id={"gx": peer},
                device_id_type=MESH,
            ).start()

    def whole(source, target, send, recv, count=n - 1):
        others = pl.ds(0, count)
        return pltpu.make_async_remote_copy(
            src_ref=source(others),
            dst_ref=target(others),
            send_sem=send,
            recv_sem=recv,
            device_id={"gx": lax.rem(me + 1, n)},
            device_id_type=MESH,
        )

    index_args = (lambda p: index_rows.at[p], lambda p: got_index.at[p], remote_sems.at[0], remote_sems.at[1])

    def spans(at):
        return sum(GROUPS[:at]) // quad, sum(GROUPS[: at + 1]) // quad

    def piece_args(at, side):
        first, last = spans(at)
        span = pl.ds(first * LANES, (last - first) * LANES)
        return (
            lambda p: spec.at[p, :, span], lambda p: got_spec.at[p, :, span],
            remote_sems.at[2], spec_sems.at[at, side],
        )

    def beam_args(h):
        return (
            lambda p: sending.at[h, p], lambda p: got_beams.at[h, p],
            remote_sems.at[3], remote_sems.at[4 + h],
        )

    load_taps.wait()
    for tap in range(TAP_COUNT):
        wide_taps[tap] = jnp.broadcast_to(taps[tap : tap + 1, :], (SUBLANES, FORWARD_LENGTH)).astype(jnp.bfloat16)

    def filtered(at, k):
        span = slice(k * K_TILE, (k + 1) * K_TILE)
        tap = [wide_taps[j, :, span] for j in range(TAP_COUNT)]
        first = sum(GROUPS[:at])
        pieces = []
        for block in range(antennas // SUBLANES):
            x = [
                volts[
                    block * SUBLANES : (block + 1) * SUBLANES,
                    f * FORWARD_LENGTH + k * K_TILE : f * FORWARD_LENGTH + (k + 1) * K_TILE,
                ]
                for f in range(first, first + GROUPS[at] + TAP_COUNT - 1)
            ]
            pieces.append(
                [
                    (x[f] * tap[0] + x[f + 1] * tap[1]) + (x[f + 2] * tap[2] + x[f + 3] * tap[3])
                    for f in range(GROUPS[at])
                ]
            )
        return jnp.concatenate([piece[f] for f in range(GROUPS[at]) for piece in pieces], 0)

    def emit(at, total):
        first, last = spans(at)
        kept = jnp.concatenate([keep[...]] * (last - first), 1)
        spec[:, :, first * LANES : last * LANES] = (total * kept).reshape(n, parts, (last - first) * LANES).astype(
            jnp.bfloat16
        )

    def small():
        load_index.wait()
        load_flagged.wait()
        lane_one = lax.broadcasted_iota(jnp.int32, (1, LANES), 1) % antennas
        row = jnp.zeros((1, LANES), jnp.int32)
        for a in range(antennas):
            row = jnp.where(lane_one == a, index[a], row)
        index_rows[...] = jnp.broadcast_to(row[None], index_rows.shape)
        off = jnp.zeros((1, LANES), jnp.int32)
        for a in range(antennas):
            off = jnp.where(lane_one == a, flagged[a], off)
        keep[...] = (1 - off).astype(jnp.float32) * FORWARD_LENGTH ** (-0.5)

    def turn():
        load_trials.wait()
        beam = lax.broadcasted_iota(jnp.int32, (beams, LANES), 0)
        trial = jnp.zeros((beams, LANES), jnp.int32)
        for b in range(beams):
            trial = jnp.where(beam == b, trials[b], trial)
        scaled = (-2.0 * math.pi * DM_UNIT) * (trial.astype(jnp.float32) + 1.0)
        lane = lax.broadcasted_iota(jnp.int32, (n, beams, LANES), 2)
        owner = lax.broadcasted_iota(jnp.int32, (n, beams, LANES), 0)
        chan = (owner * locals_ + lane // half % locals_).astype(jnp.float32) / channels
        phase = scaled[None] * (chan * chan)
        chirp[0] = jnp.cos(phase)
        chirp[1] = jnp.where(lane < LANES // 2, -1.0, 1.0) * jnp.sin(phase)

    def gather_weights():
        whole(*index_args).wait_recv()
        load_weights.wait()
        lane = lax.broadcasted_iota(jnp.int32, (LANES, LANES), 1)
        lane_quad = lax.broadcasted_iota(jnp.int32, (1, LANES), 1) // antennas
        blocks = []
        for ag in range(n // quad):
            row = got_index[ag * quad]
            for q in range(1, quad):
                row = jnp.where(lane_quad == q, got_index[ag * quad + q], row)
            column = jnp.broadcast_to(row.astype(jnp.float32), (LANES, LANES)).T.astype(jnp.int32)
            blocks.append(
                jnp.concatenate(
                    [
                        jnp.where(column == lane + t * LANES, 1.0, 0.0).astype(jnp.bfloat16)
                        for t in range(WEIGHT_ROWS // LANES)
                    ],
                    1,
                )
            )
        onehot = jnp.concatenate(blocks, 0)
        for c in range(locals_):
            both = jnp.concatenate([weights[0, c], weights[1, c]], 1)
            gathered[c] = jnp.dot(onehot, both, preferred_element_type=jnp.float32).astype(jnp.bfloat16)

    load_table.wait()
    for at in range(steps):
        streams[at].wait()
        if at == 0:
            small()
        sums = [None, None]
        for k in range(FORWARD_LENGTH // K_TILE):
            y = filtered(at, k)
            middle = y.shape[0] // 2
            for i in range(2):
                part = lax.dot_general(
                    table[:, k * K_TILE : (k + 1) * K_TILE], y[i * middle : (i + 1) * middle], NT,
                    preferred_element_type=jnp.float32,
                )
                sums[i] = part if sums[i] is None else sums[i] + part
        total = jnp.concatenate(sums, 1)
        emit(at, total)

        @pl.when(me >= 0)
        def _():
            if at == 0:
                pl.semaphore_wait(barrier, n - 1)
                copies(*index_args)
                got_index[me] = index_rows[0]
            copies(*piece_args(at, mine))

    turn()
    got_spec[me] = spec[me]
    gather_weights()

    lane_part = lax.broadcasted_iota(jnp.int32, (parts, LANES), 1) // antennas

    def line(at, side):
        count = n // 2 if side is yours else n // 2 - 1
        whole(*piece_args(at, side), count).wait_recv()
        planes = n // quad // 2
        for sg in [side * planes + i for i in range(planes)]:
            for ft in range(*spans(at)):
                pieces = [
                    got_spec[sg * quad + s, :, ft * LANES : (ft + 1) * LANES].astype(jnp.float32)
                    for s in range(quad)
                ]
                for f in range(quad):
                    made = None
                    for s in range(quad):
                        piece = pieces[s]
                        if s != f:
                            piece = pltpu.roll(piece, ((s - f) * antennas) % LANES, 1)
                        made = piece if made is None else jnp.where(lane_part == s, piece, made)
                    to = (ft * quad + f) * parts
                    lined[sg, to : to + parts, :] = made

    def product(h, side):
        planes = n // quad // 2
        deep = planes * LANES
        made = []
        for c in range(locals_):
            left = jnp.concatenate(
                [
                    jnp.concatenate(
                        [
                            lined[side * planes + i, pl.ds(h * half * parts + r * locals_ + c, half, stride=parts), :]
                            for i in range(planes)
                        ],
                        1,
                    )
                    for r in range(2)
                ],
                0,
            ).astype(jnp.bfloat16)
            right = gathered[c, pl.ds(pl.multiple_of(side * deep, deep), deep), :]
            made.append(jnp.dot(left, right, preferred_element_type=jnp.float32))
        return made

    def spread(h, made):
        real = [both[:half, :beam_total] - both[half:, beam_total:] for both in made]
        imag = [both[:half, beam_total:] + both[half:, :beam_total] for both in made]
        stack = jnp.concatenate(real + imag, 0)
        owners = LANES // beams
        for bt in range(beam_total // LANES):
            across = stack[:, bt * LANES : (bt + 1) * LANES].T
            sending[h, bt * owners : (bt + 1) * owners] = across.reshape(owners, beams, LANES).astype(jnp.bfloat16)

    def finish(h):
        whole(*beam_args(h)).wait_recv()
        for s in range(n):
            block = got_beams[h, s].astype(jnp.float32)
            swapped = pltpu.roll(block, LANES // 2, 1)
            turned[pl.ds(s, beams, stride=n), :] = block * chirp[0, s] + swapped * chirp[1, s]
        each = LANES // n
        deep = parts // each
        place = lax.broadcasted_iota(jnp.int32, (half, LANES), 1) // n
        masks = [jnp.where(place == slot, 1.0, 0.0).astype(jnp.bfloat16) for slot in range(each)]
        left = []
        for g in range(beams // each):
            across = turned[g * LANES : (g + 1) * LANES, :].T.astype(jnp.bfloat16)
            for b in range(each):
                tiles = []
                for k in range(deep):
                    made = None
                    for slot in range(each):
                        piece = across[(k * each + slot) * half : (k * each + slot + 1) * half]
                        if b != slot:
                            piece = pltpu.roll(piece, ((slot - b) * n) % LANES, 1)
                        piece = piece * masks[slot]
                        made = piece if made is None else made + piece
                    tiles.append(made)
                left.append(jnp.concatenate(tiles, 1))
        left = jnp.concatenate(left, 0)
        for s in range(2):
            total = jnp.dot(left, inverse[s], preferred_element_type=jnp.float32) * channels ** (-0.5)
            for b in range(beams):
                out[s, h * half : (h + 1) * half, b, :] = total[b * half : (b + 1) * half]

    done = 0
    for h in range(halves):
        while sum(GROUPS[: done + 1]) < (h + 1) * half:
            line(done, mine)
            line(done, yours)
            done += 1
        line(done, mine)
        for c, both in enumerate(product(h, mine)):
            partial[c] = both
        line(done, yours)
        far = product(h, yours)
        done += 1
        spread(h, [partial[c] + both for c, both in enumerate(far)])
        copies(*beam_args(h))
        got_beams[h, me] = sending[h, me]
    load_inverse.wait()
    whole(*index_args).wait_send()
    whole(lambda p: spec.at[p], lambda p: got_spec.at[p], remote_sems.at[2], remote_sems.at[1]).wait_send()
    for h in range(halves):
        finish(h)
    whole(
        lambda p: sending.at[:, p], lambda p: got_beams.at[:, p], remote_sems.at[3], remote_sems.at[4]
    ).wait_send()


def per_device(voltages, taps, weights, antenna_weight_index, flagged, trials):
    n = lax.axis_size("gx")
    locals_ = weights.shape[1]
    beam_total = weights.shape[3]
    channels = locals_ * n
    antennas = voltages.shape[0]
    beams = trials.shape[0]
    parts = 2 * locals_
    rows = 2 * channels
    half = LANES // parts
    halves = FRAME_COUNT // half
    steps = len(GROUPS)
    table = forward_rows(channels, n)
    inverse = inverse_rows(channels, n)
    room = 2 * FRAME_COUNT * beams * max(channels, LANES) * 4 + (1 << 17)
    hbm = pl.BlockSpec(memory_space=pltpu.HBM)
    return pl.pallas_call(
        functools.partial(kernel, n),
        out_shape=pltpu.VMEM((2, FRAME_COUNT, beams, channels), jnp.float32),
        in_specs=[hbm] * 8,
        out_specs=pl.BlockSpec(memory_space=pltpu.VMEM),
        scratch_shapes=[
            pltpu.SMEM(antenna_weight_index.shape, jnp.int32),
            pltpu.SMEM(flagged.shape, jnp.int32),
            pltpu.SMEM(trials.shape, jnp.int32),
            pltpu.VMEM(voltages.shape, jnp.bfloat16),
            pltpu.VMEM(taps.shape, jnp.float32),
            pltpu.VMEM(table.shape, jnp.bfloat16),
            pltpu.VMEM(weights.shape, jnp.bfloat16),
            pltpu.VMEM(inverse.shape, jnp.bfloat16),
            pltpu.VMEM((TAP_COUNT, SUBLANES, FORWARD_LENGTH), jnp.bfloat16),
            pltpu.VMEM((1, LANES), jnp.float32),
            pltpu.VMEM((2, n, beams, LANES), jnp.float32),
            pltpu.VMEM((n, 1, LANES), jnp.int32),
            pltpu.VMEM((n, parts, FRAME_COUNT * antennas), jnp.bfloat16),
            pltpu.VMEM((n, 1, LANES), jnp.int32),
            pltpu.VMEM((n, parts, FRAME_COUNT * antennas), jnp.bfloat16),
            pltpu.VMEM((locals_, n * antennas, 2 * beam_total), jnp.bfloat16),
            pltpu.VMEM((locals_, 2 * half, 2 * beam_total), jnp.float32),
            pltpu.VMEM((n * antennas // LANES, FRAME_COUNT * parts, LANES), jnp.float32),
            pltpu.VMEM((halves, n, beams, LANES), jnp.bfloat16),
            pltpu.VMEM((halves, n, beams, LANES), jnp.bfloat16),
            pltpu.VMEM((beams * n, LANES), jnp.float32),
            pltpu.SemaphoreType.DMA((steps + 7,)),
            pltpu.SemaphoreType.DMA((4 + halves,)),
            pltpu.SemaphoreType.DMA((steps, 2)),
        ],
        compiler_params=pltpu.CompilerParams(
            collective_id=0, has_side_effects=True, vmem_limit_bytes=VMEM_BYTES - room
        ),
        name="beamformer",
    )(
        antenna_weight_index, flagged, trials, voltages, taps,
        jnp.asarray(table), weights, jnp.asarray(inverse),
    )


def solution(mesh):
    return jax.shard_map(
        per_device,
        mesh=mesh,
        in_specs=(
            P(("grp", "gx"), None),
            P(),
            P(None, "gx", None, None),
            P(("grp", "gx")),
            P(("grp", "gx")),
            P(("grp", "gx")),
        ),
        out_specs=P(None, None, ("grp", "gx"), None),
        check_vma=False,
    )
```

```python
import functools
import math

import jax
import jax.numpy as jnp
import numpy as np
from jax import lax
from jax.experimental import pallas as pl
from jax.experimental.pallas import tpu as pltpu
from jax.sharding import PartitionSpec as P

FRAME_COUNT = 32
FORWARD_LENGTH = 4096
TAP_COUNT = 4
CH_LO = 1024
WEIGHT_ROWS = 256
LANES = 128
SUBLANES = 16
DM_UNIT = 0.173
MESH = pl.DeviceIdType.MESH
NT = (((1,), (1,)), ((), ()))
VMEM_BYTES = 67108864
GROUPS = (8, 8, 8, 8)
K_TILE = 256
LATE = 1


def forward_rows(channels, owners):
    local = channels // owners
    kept = np.arange(channels).reshape(owners, 1, local)
    bins = np.broadcast_to(CH_LO + kept, (owners, 2, local)).reshape(-1)
    part = np.broadcast_to(np.arange(2).reshape(1, 2, 1), (owners, 2, local)).reshape(-1)
    angle = (bins[:, None] * np.arange(FORWARD_LENGTH)[None] % FORWARD_LENGTH) * (2.0 * math.pi / FORWARD_LENGTH)
    return np.where(part[:, None] == 0, np.cos(angle), -np.sin(angle)).astype(jnp.bfloat16)


def inverse_rows(channels, owners):
    local = channels // owners
    chan = (np.arange(owners)[None, :] * local + np.arange(local)[:, None]).reshape(1, -1, 1)
    angle = (chan * np.arange(channels) % channels) * (2.0 * math.pi / channels)
    cosine, sine = np.cos(angle), np.sin(angle)
    real = np.concatenate([cosine, -sine], 0)
    imag = np.concatenate([sine, cosine], 0)
    return np.stack([real, imag]).reshape(2, 2 * channels, channels).astype(jnp.bfloat16)


def kernel(
    n, index_hbm, flagged_hbm, trials_hbm, volts_hbm, taps_hbm, table_hbm, weights_hbm, inverse_hbm, out,
    index, flagged, trials, volts, taps, table, weights, inverse,
    wide_taps, keep, chirp, index_rows, spec,
    got_index, got_spec, gathered, partial, lined, sending, got_beams, turned,
    load_sems, remote_sems, spec_sems,
):
    me = lax.axis_index("gx")
    mine = me // (n // 2)
    yours = 1 - mine
    antennas = volts.shape[0]
    locals_ = weights.shape[1]
    beam_total = weights.shape[3]
    channels = n * locals_
    rows = 2 * channels
    frames = FRAME_COUNT
    quad = LANES // antennas
    parts = 2 * locals_
    half = LANES // parts
    halves = frames // half
    beams = beam_total // n
    steps = len(GROUPS)

    enter = LATE * (1 - lax.min(me // (3 * n // 8), 1))
    barrier = pltpu.get_barrier_semaphore()
    for d in range(1, n):
        pl.semaphore_signal(barrier, inc=1, device_id={"gx": lax.rem(me + d, n)}, device_id_type=MESH)

    def load(source, target, at):
        return pltpu.make_async_copy(source, target, load_sems.at[at])

    streams = []
    for at in range(steps):
        begin = sum(GROUPS[:at]) + (TAP_COUNT - 1 if at else 0)
        end = sum(GROUPS[: at + 1]) + TAP_COUNT - 1
        span = pl.ds(begin * FORWARD_LENGTH, (end - begin) * FORWARD_LENGTH)
        streams.append(load(volts_hbm.at[:, span], volts.at[:, span], at))
    load_taps = load(taps_hbm, taps, steps)
    load_table = load(table_hbm, table, steps + 1)
    load_weights = load(weights_hbm, weights, steps + 2)
    load_inverse = load(inverse_hbm, inverse, steps + 3)
    load_index = load(index_hbm, index, steps + 4)
    load_flagged = load(flagged_hbm, flagged, steps + 5)
    load_trials = load(trials_hbm, trials, steps + 6)
    for one in (load_taps, load_table, streams[0], load_index, load_flagged, load_trials):
        one.start()
    for one in streams[1:] + [load_weights, load_inverse]:
        one.start()
    peers = [lax.rem(me + d, n) for d in range(n)]

    def copies(source, target, send, recv):
        for peer in peers[1:]:
            pltpu.make_async_remote_copy(
                src_ref=source(peer),
                dst_ref=target(me),
                send_sem=send,
                recv_sem=recv,
                device_id={"gx": peer},
                device_id_type=MESH,
            ).start()

    def whole(source, target, send, recv, count=n - 1):
        others = pl.ds(0, count)
        return pltpu.make_async_remote_copy(
            src_ref=source(others),
            dst_ref=target(others),
            send_sem=send,
            recv_sem=recv,
            device_id={"gx": lax.rem(me + 1, n)},
            device_id_type=MESH,
        )

    index_args = (lambda p: index_rows.at[p], lambda p: got_index.at[p], remote_sems.at[0], remote_sems.at[1])

    def spans(at):
        return sum(GROUPS[:at]) // quad, sum(GROUPS[: at + 1]) // quad

    def piece_args(at, side):
        first, last = spans(at)
        span = pl.ds(first * LANES, (last - first) * LANES)
        return (
            lambda p: spec.at[p, :, span], lambda p: got_spec.at[p, :, span],
            remote_sems.at[2], spec_sems.at[at, side],
        )

    def beam_args(h):
        return (
            lambda p: sending.at[h, p], lambda p: got_beams.at[h, p],
            remote_sems.at[3], remote_sems.at[4 + h],
        )

    load_taps.wait()
    for tap in range(TAP_COUNT):
        wide_taps[tap] = jnp.broadcast_to(taps[tap : tap + 1, :], (SUBLANES, FORWARD_LENGTH)).astype(jnp.bfloat16)

    def filtered(at, k):
        span = slice(k * K_TILE, (k + 1) * K_TILE)
        tap = [wide_taps[j, :, span] for j in range(TAP_COUNT)]
        first = sum(GROUPS[:at])
        pieces = []
        for block in range(antennas // SUBLANES):
            x = [
                volts[
                    block * SUBLANES : (block + 1) * SUBLANES,
                    f * FORWARD_LENGTH + k * K_TILE : f * FORWARD_LENGTH + (k + 1) * K_TILE,
                ]
                for f in range(first, first + GROUPS[at] + TAP_COUNT - 1)
            ]
            pieces.append(
                [
                    (x[f] * tap[0] + x[f + 1] * tap[1]) + (x[f + 2] * tap[2] + x[f + 3] * tap[3])
                    for f in range(GROUPS[at])
                ]
            )
        return jnp.concatenate([piece[f] for f in range(GROUPS[at]) for piece in pieces], 0)

    def emit(at, total):
        first, last = spans(at)
        kept = jnp.concatenate([keep[...]] * (last - first), 1)
        spec[:, :, first * LANES : last * LANES] = (total * kept).reshape(n, parts, (last - first) * LANES).astype(
            jnp.bfloat16
        )

    def small():
        load_index.wait()
        load_flagged.wait()
        lane_one = lax.broadcasted_iota(jnp.int32, (1, LANES), 1) % antennas
        row = jnp.zeros((1, LANES), jnp.int32)
        for a in range(antennas):
            row = jnp.where(lane_one == a, index[a], row)
        index_rows[...] = jnp.broadcast_to(row[None], index_rows.shape)
        off = jnp.zeros((1, LANES), jnp.int32)
        for a in range(antennas):
            off = jnp.where(lane_one == a, flagged[a], off)
        keep[...] = (1 - off).astype(jnp.float32) * FORWARD_LENGTH ** (-0.5)

    def turn():
        load_trials.wait()
        beam = lax.broadcasted_iota(jnp.int32, (beams, LANES), 0)
        trial = jnp.zeros((beams, LANES), jnp.int32)
        for b in range(beams):
            trial = jnp.where(beam == b, trials[b], trial)
        scaled = (-2.0 * math.pi * DM_UNIT) * (trial.astype(jnp.float32) + 1.0)
        lane = lax.broadcasted_iota(jnp.int32, (n, beams, LANES), 2)
        owner = lax.broadcasted_iota(jnp.int32, (n, beams, LANES), 0)
        chan = (owner * locals_ + lane // half % locals_).astype(jnp.float32) / channels
        phase = scaled[None] * (chan * chan)
        chirp[0] = jnp.cos(phase)
        chirp[1] = jnp.where(lane < LANES // 2, -1.0, 1.0) * jnp.sin(phase)

    def gather_weights():
        whole(*index_args).wait_recv()
        load_weights.wait()
        lane = lax.broadcasted_iota(jnp.int32, (LANES, LANES), 1)
        lane_quad = lax.broadcasted_iota(jnp.int32, (1, LANES), 1) // antennas
        blocks = []
        for ag in range(n // quad):
            row = got_index[ag * quad]
            for q in range(1, quad):
                row = jnp.where(lane_quad == q, got_index[ag * quad + q], row)
            column = jnp.broadcast_to(row.astype(jnp.float32), (LANES, LANES)).T.astype(jnp.int32)
            blocks.append(
                jnp.concatenate(
                    [
                        jnp.where(column == lane + t * LANES, 1.0, 0.0).astype(jnp.bfloat16)
                        for t in range(WEIGHT_ROWS // LANES)
                    ],
                    1,
                )
            )
        onehot = jnp.concatenate(blocks, 0)
        for c in range(locals_):
            both = jnp.concatenate([weights[0, c], weights[1, c]], 1)
            gathered[c] = jnp.dot(onehot, both, preferred_element_type=jnp.float32).astype(jnp.bfloat16)

    load_table.wait()
    for at in range(steps):
        streams[at].wait()
        if at == 0:
            small()
        sums = [None, None]
        for k in range(FORWARD_LENGTH // K_TILE):
            y = filtered(at, k)
            middle = y.shape[0] // 2
            for i in range(2):
                part = lax.dot_general(
                    table[:, k * K_TILE : (k + 1) * K_TILE], y[i * middle : (i + 1) * middle], NT,
                    preferred_element_type=jnp.float32,
                )
                sums[i] = part if sums[i] is None else sums[i] + part
        total = jnp.concatenate(sums, 1)
        emit(at, total)

        if at in (0, LATE):
            @pl.when(enter == at)
            def _():
                pl.semaphore_wait(barrier, n - 1)
                copies(*index_args)
                got_index[me] = index_rows[0]
                for earlier in range(at):
                    copies(*piece_args(earlier, mine))

        @pl.when(enter <= at)
        def _():
            copies(*piece_args(at, mine))

    turn()
    got_spec[me] = spec[me]
    gather_weights()

    lane_part = lax.broadcasted_iota(jnp.int32, (parts, LANES), 1) // antennas

    def line(at, side):
        count = n // 2 if side is yours else n // 2 - 1
        whole(*piece_args(at, side), count).wait_recv()
        planes = n // quad // 2
        for sg in [side * planes + i for i in range(planes)]:
            for ft in range(*spans(at)):
                pieces = [
                    got_spec[sg * quad + s, :, ft * LANES : (ft + 1) * LANES].astype(jnp.float32)
                    for s in range(quad)
                ]
                for f in range(quad):
                    made = None
                    for s in range(quad):
                        piece = pieces[s]
                        if s != f:
                            piece = pltpu.roll(piece, ((s - f) * antennas) % LANES, 1)
                        made = piece if made is None else jnp.where(lane_part == s, piece, made)
                    to = (ft * quad + f) * parts
                    lined[sg, to : to + parts, :] = made

    def product(h, side):
        planes = n // quad // 2
        deep = planes * LANES
        made = []
        for c in range(locals_):
            left = jnp.concatenate(
                [
                    jnp.concatenate(
                        [
                            lined[side * planes + i, pl.ds(h * half * parts + r * locals_ + c, half, stride=parts), :]
                            for i in range(planes)
                        ],
                        1,
                    )
                    for r in range(2)
                ],
                0,
            ).astype(jnp.bfloat16)
            right = gathered[c, pl.ds(pl.multiple_of(side * deep, deep), deep), :]
            made.append(jnp.dot(left, right, preferred_element_type=jnp.float32))
        return made

    def spread(h, made):
        real = [both[:half, :beam_total] - both[half:, beam_total:] for both in made]
        imag = [both[:half, beam_total:] + both[half:, :beam_total] for both in made]
        stack = jnp.concatenate(real + imag, 0)
        owners = LANES // beams
        for bt in range(beam_total // LANES):
            across = stack[:, bt * LANES : (bt + 1) * LANES].T
            sending[h, bt * owners : (bt + 1) * owners] = across.reshape(owners, beams, LANES).astype(jnp.bfloat16)

    def finish(h):
        whole(*beam_args(h)).wait_recv()
        for s in range(n):
            block = got_beams[h, s].astype(jnp.float32)
            swapped = pltpu.roll(block, LANES // 2, 1)
            turned[pl.ds(s, beams, stride=n), :] = block * chirp[0, s] + swapped * chirp[1, s]
        each = LANES // n
        deep = parts // each
        place = lax.broadcasted_iota(jnp.int32, (half, LANES), 1) // n
        masks = [jnp.where(place == slot, 1.0, 0.0).astype(jnp.bfloat16) for slot in range(each)]
        left = []
        for g in range(beams // each):
            across = turned[g * LANES : (g + 1) * LANES, :].T.astype(jnp.bfloat16)
            for b in range(each):
                tiles = []
                for k in range(deep):
                    made = None
                    for slot in range(each):
                        piece = across[(k * each + slot) * half : (k * each + slot + 1) * half]
                        if b != slot:
                            piece = pltpu.roll(piece, ((slot - b) * n) % LANES, 1)
                        piece = piece * masks[slot]
                        made = piece if made is None else made + piece
                    tiles.append(made)
                left.append(jnp.concatenate(tiles, 1))
        left = jnp.concatenate(left, 0)
        for s in range(2):
            total = jnp.dot(left, inverse[s], preferred_element_type=jnp.float32) * channels ** (-0.5)
            for b in range(beams):
                out[s, h * half : (h + 1) * half, b, :] = total[b * half : (b + 1) * half]

    done = 0
    for h in range(halves):
        while sum(GROUPS[: done + 1]) < (h + 1) * half:
            line(done, mine)
            line(done, yours)
            done += 1
        line(done, mine)
        for c, both in enumerate(product(h, mine)):
            partial[c] = both
        line(done, yours)
        far = product(h, yours)
        done += 1
        spread(h, [partial[c] + both for c, both in enumerate(far)])
        copies(*beam_args(h))
        got_beams[h, me] = sending[h, me]
    load_inverse.wait()
    whole(*index_args).wait_send()
    whole(lambda p: spec.at[p], lambda p: got_spec.at[p], remote_sems.at[2], remote_sems.at[1]).wait_send()
    for h in range(halves):
        finish(h)
    whole(
        lambda p: sending.at[:, p], lambda p: got_beams.at[:, p], remote_sems.at[3], remote_sems.at[4]
    ).wait_send()


def per_device(voltages, taps, weights, antenna_weight_index, flagged, trials):
    n = lax.axis_size("gx")
    locals_ = weights.shape[1]
    beam_total = weights.shape[3]
    channels = locals_ * n
    antennas = voltages.shape[0]
    beams = trials.shape[0]
    parts = 2 * locals_
    rows = 2 * channels
    half = LANES // parts
    halves = FRAME_COUNT // half
    steps = len(GROUPS)
    table = forward_rows(channels, n)
    inverse = inverse_rows(channels, n)
    room = 2 * FRAME_COUNT * beams * max(channels, LANES) * 4 + (1 << 17)
    hbm = pl.BlockSpec(memory_space=pltpu.HBM)
    return pl.pallas_call(
        functools.partial(kernel, n),
        out_shape=pltpu.VMEM((2, FRAME_COUNT, beams, channels), jnp.float32),
        in_specs=[hbm] * 8,
        out_specs=pl.BlockSpec(memory_space=pltpu.VMEM),
        scratch_shapes=[
            pltpu.SMEM(antenna_weight_index.shape, jnp.int32),
            pltpu.SMEM(flagged.shape, jnp.int32),
            pltpu.SMEM(trials.shape, jnp.int32),
            pltpu.VMEM(voltages.shape, jnp.bfloat16),
            pltpu.VMEM(taps.shape, jnp.float32),
            pltpu.VMEM(table.shape, jnp.bfloat16),
            pltpu.VMEM(weights.shape, jnp.bfloat16),
            pltpu.VMEM(inverse.shape, jnp.bfloat16),
            pltpu.VMEM((TAP_COUNT, SUBLANES, FORWARD_LENGTH), jnp.bfloat16),
            pltpu.VMEM((1, LANES), jnp.float32),
            pltpu.VMEM((2, n, beams, LANES), jnp.float32),
            pltpu.VMEM((n, 1, LANES), jnp.int32),
            pltpu.VMEM((n, parts, FRAME_COUNT * antennas), jnp.bfloat16),
            pltpu.VMEM((n, 1, LANES), jnp.int32),
            pltpu.VMEM((n, parts, FRAME_COUNT * antennas), jnp.bfloat16),
            pltpu.VMEM((locals_, n * antennas, 2 * beam_total), jnp.bfloat16),
            pltpu.VMEM((locals_, 2 * half, 2 * beam_total), jnp.float32),
            pltpu.VMEM((n * antennas // LANES, FRAME_COUNT * parts, LANES), jnp.float32),
            pltpu.VMEM((halves, n, beams, LANES), jnp.bfloat16),
            pltpu.VMEM((halves, n, beams, LANES), jnp.bfloat16),
            pltpu.VMEM((beams * n, LANES), jnp.float32),
            pltpu.SemaphoreType.DMA((steps + 7,)),
            pltpu.SemaphoreType.DMA((4 + halves,)),
            pltpu.SemaphoreType.DMA((steps, 2)),
        ],
        compiler_params=pltpu.CompilerParams(
            collective_id=0, has_side_effects=True, vmem_limit_bytes=VMEM_BYTES - room
        ),
        name="beamformer",
    )(
        antenna_weight_index, flagged, trials, voltages, taps,
        jnp.asarray(table), weights, jnp.asarray(inverse),
    )


def solution(mesh):
    return jax.shard_map(
        per_device,
        mesh=mesh,
        in_specs=(
            P(("grp", "gx"), None),
            P(),
            P(None, "gx", None, None),
            P(("grp", "gx")),
            P(("grp", "gx")),
            P(("grp", "gx")),
        ),
        out_specs=P(None, None, ("grp", "gx"), None),
        check_vma=False,
    )
```
